32 devices in a mesh: group: 4 (over y, x), expert: 8 (over z, core).
Axes of the slice: x: 2, y: 2, z: 4, core: 2. Of those that a mesh axis runs over, the one named last changes fastest.
Arguments:
- residual_in: bfloat16 [4096, 2560], P(('group', 'expert')), may hold values from -3 to 3
- queries: bfloat16 [4096, 2560], P(('group', 'expert')), may hold values from -8 to 8
- suffix_key_rows: bfloat16 [4096, 512], P(('group', 'expert')), may hold values from -8 to 8
- suffix_value_rows: bfloat16 [4096, 512], P(('group', 'expert')), may hold values from -6 to 6
- cached_prefix_keys: bfloat16 [4096, 512], P(('group', 'expert')), may hold values from -6 to 6
- cached_prefix_values: bfloat16 [4096, 512], P(('group', 'expert')), may hold values from -6 to 6
- suffix_length_list: int32 [4, 8], replicated, may hold values from 1 to 512, 1024 in all within a row
- prefix_read_flags: int32 [4, 8], replicated, may hold values 0 or 1
- attn_out_weight: bfloat16 [2560, 2560], replicated, may hold values from -0.3125 to 0.3125
- norm_gain: float32 [2560], replicated, may hold values from 0.1 to 1.9
- routes: int32 [4096, 6], P(('group', 'expert')), may hold values from 0 to 15, all different within a row; in each aligned block of 128 rows (0 to 127, 128 to 255, ...) at most 64 rows name the same one
- route_weights: float32 [4096, 6], P(('group', 'expert')), may hold values from 0.1 to 1
- expert_gate: bfloat16 [32, 512, 2560], P(('group', 'expert')), may hold values from -0.125 to 0.125
- expert_up: bfloat16 [32, 512, 2560], P(('group', 'expert')), may hold values from -0.125 to 0.125
- expert_down: bfloat16 [32, 512, 2560], P(('group', 'expert')), may hold values from -0.1875 to 0.1875
Outputs:
- layer_out: bfloat16 [4096, 2560], P(('group', 'expert'))
The draws below stay inside these ranges and needn't reach their ends.
Inputs may be any that keep to these rules, and one draw needn't show every extreme that they name: `suffix_length_list`: the lengths of each group sum to 1024. `routes`: within each aligned block of 128 rows no expert is named by more than 64 rows, and in every draw some block names some expert exactly 64 times.
All inputs are finite; a program needn't handle non-finite values.
Results may differ from the reference program's by a relative error of at most 0.0085.
Values may be sent and summed in bfloat16 or wider, within the bound.
A program may use at most 192 MiB of HBM per device.

```python
import math
import jax
import jax.numpy as jnp
import numpy as np
from jax import lax

D = 2560
QUERY_HEADS = 20
KEY_VALUE_HEADS = 4
HEAD_SIZE = 128
GRP = 5
FFE = 1024
FFH = 512
TOP = 6
TOK_DEV = 128
REQS = 8
EXPERTS = 16
SUFFIX_TOKENS = 1024
TOKEN_TOTAL = 4096
PREFIX_TOKENS = 1024
CAP = 64
N_GROUP = 4
DEVICES = 32


def draw_queries(key, part):
    value_matrix = 2.0 * jax.random.truncated_normal(jax.random.fold_in(key, 1), -3.0, 3.0, (TOKEN_TOTAL, QUERY_HEADS * HEAD_SIZE), jnp.float32)
    return value_matrix.astype(jnp.bfloat16)


def draw_suffix_key_rows(key, part):
    value_matrix = jax.random.truncated_normal(jax.random.fold_in(key, 2), -6.0, 6.0, (TOKEN_TOTAL, KEY_VALUE_HEADS * HEAD_SIZE), jnp.float32)
    return value_matrix.astype(jnp.bfloat16)


def place_ends(values, stream_key, least, high):
    extent = values.shape
    place = [jax.random.randint(jax.random.fold_in(stream_key, axis), (), 0, extent[axis]) for axis in range(len(extent))]
    values = values.at[tuple(place)].set(least)
    longest = extent.index(max(extent))
    place[longest] = (place[longest] + 1) % extent[longest]
    return values.at[tuple(place)].set(high)


def shard_levels(rng, extent, pieces, low, high):
    level, own = 1.0, jax.random.fold_in(rng, 6)
    for dim, blocks in pieces:
        draws = jnp.exp(jax.random.uniform(jax.random.fold_in(own, dim), (blocks,), jnp.float32, low / len(pieces), high / len(pieces)))
        level = level * jnp.repeat(draws, extent[dim] // blocks).reshape([-1 if axis == dim else 1 for axis in range(len(extent))])
    return level


def split_up(amount, total, reach, slope):
    loads = [(1 << 20) // math.isqrt(standing ** slope) + 1 for standing in range(2, amount + 1)]
    surplus, holding = total - reach - (amount - 1), [1] * (amount - 1)
    while surplus > 0:
        candidates = [i for i in range(amount - 1) if holding[i] < reach]
        whole, remaining = sum([loads[i] for i in candidates]), surplus
        for i in candidates:
            more = min(reach - holding[i], max(1, remaining * loads[i] // whole), surplus)
            holding[i] = holding[i] + more
            surplus = surplus - more
    return np.array([reach] + holding)


def uneven(rng, amount, total, bound, lean):
    if amount == 2:
        one = jax.random.randint(rng, (), max(1, total - bound), min(bound, total - 1) + 1)
        return jnp.stack([one, total - one])
    tallies = jnp.asarray(split_up(amount, total, bound, lean), jnp.int32)
    twos = (amount - 1) // 2
    source_of, sink = tallies[1:1 + 2 * twos:2], tallies[2:2 + 2 * twos:2]
    room = jnp.minimum(source_of - 1, bound - sink)
    passed = jax.random.randint(jax.random.fold_in(rng, 1), (twos,), 0, 1 << 20) % (room + 1)
    tallies = tallies.at[1:1 + 2 * twos:2].set(source_of - passed).at[2:2 + 2 * twos:2].set(sink + passed)
    return tallies[jax.random.permutation(jax.random.fold_in(rng, 2), amount)]


def deal_out(stream_key, own, number, rows, count, top, reach, skew):
    order = jax.random.permutation(stream_key, count)
    crowded, ordinary = load_shares(count, rows * top, reach, skew, True), load_shares(count, rows * top, reach, skew, False)
    places = jnp.arange(count)

    def named(tallies, turn):
        used = int((tallies > 0).sum())
        fixed = max(1, used // 4)
        moved = fixed + (places - fixed + turn * (used - fixed)) % max(1, count - fixed)
        return jnp.zeros((count,), jnp.int32).at[order[jnp.where(places < fixed, places, moved)]].set(jnp.asarray(tallies, jnp.int32))

    tallies = jnp.where(number % 4 == 0, named(crowded, number // 4), named(ordinary, number - number // 4 - 1))
    mixed = jax.random.permutation(jax.random.fold_in(own, 3), count)
    giver, receiver = mixed[0:count // 2 * 2:2], mixed[1:count // 2 * 2:2]
    room = jnp.minimum(tallies[giver] - 1, reach - tallies[receiver]) // 2
    room = jnp.where((giver == order[0]) | (receiver == order[0]) | (tallies[receiver] == 0), 0, jnp.maximum(room, 0))
    moved = jax.random.randint(jax.random.fold_in(own, 4), (count // 2,), 0, 1 << 20) % (room + 1)
    tallies = tallies.at[giver].add(-moved).at[receiver].add(moved)
    labels = jnp.searchsorted(jnp.cumsum(tallies), jnp.arange(rows * top), side="right").astype(jnp.int32)
    table = labels.reshape(top, rows).T
    table = table[jax.random.permutation(jax.random.fold_in(own, 1), rows)]
    turn = jax.random.randint(jax.random.fold_in(own, 2), (rows, 1), 0, top)
    return jnp.take_along_axis(table, (jnp.arange(top)[None, :] + turn) % top, axis=1)


def load_shares(number_of, total, bound, slope, full):
    loads = [(1 << 20) // math.isqrt(rank ** slope) + 1 for rank in range(1, number_of + 1)]
    largest = bound if full else min(bound, max(-(-total // number_of), total * loads[0] // sum(loads)))
    least = 1 if total - largest >= number_of - 1 else 0
    given, surplus = [largest] + [least] * (number_of - 1), total - largest - least * (number_of - 1)
    while surplus > 0:
        candidates = [i for i in range(1, number_of) if given[i] < largest] or [i for i in range(1, number_of) if given[i] < bound]
        whole, budget = sum([loads[i] for i in candidates]), surplus
        for i in candidates:
            extra = min(bound - given[i], max(1, budget * loads[i] // whole), surplus)
            given[i] = given[i] + extra
            surplus = surplus - extra
    return np.array(given)


def normal_values(rng, dims, deviation, most, pieces=(), kind=jnp.bfloat16):
    result = jax.random.normal(rng, dims, jnp.float32) * deviation
    if len(pieces) > 0:
        result = shard_levels(rng, dims, pieces, -0.22, 0.18) * result
    return jnp.clip(result, min=-most, max=most).astype(kind)


def setup_inputs(seed: int = 0) -> dict:
    key_of = jax.random.split(jax.random.key(seed), 16)
    residual_in = normal_values(key_of[0], (TOKEN_TOTAL, D), 0.5, 3.0, ((0, 32),))
    queries = draw_queries(jax.random.fold_in(key_of[15], 71), 0)
    suffix_key_rows = draw_suffix_key_rows(jax.random.fold_in(key_of[15], 71), 0)
    suffix_value_rows = normal_values(key_of[3], (TOKEN_TOTAL, KEY_VALUE_HEADS * HEAD_SIZE), 1.0, 6.0, ((0, 32),))
    cached_prefix_keys = normal_values(key_of[4], (N_GROUP * PREFIX_TOKENS, KEY_VALUE_HEADS * HEAD_SIZE), 1.0, 6.0, ((0, 32),))
    cached_prefix_values = normal_values(key_of[5], (N_GROUP * PREFIX_TOKENS, KEY_VALUE_HEADS * HEAD_SIZE), 1.0, 6.0, ((0, 32),))
    suffix_length_list = jax.vmap(lambda own: uneven(own, REQS, SUFFIX_TOKENS, SUFFIX_TOKENS // 2, 2))(jax.random.split(key_of[6], N_GROUP)).reshape((N_GROUP, REQS)).astype(jnp.int32)
    prefix_read_flags = place_ends((jax.random.randint(key_of[7], (N_GROUP, REQS), 0, 4) < 3).astype(jnp.int32), jax.random.fold_in(key_of[7], 1), 0, 1)
    attn_out_weight = normal_values(key_of[8], (QUERY_HEADS * HEAD_SIZE, D), (QUERY_HEADS * HEAD_SIZE // 8) ** -0.5, 0.3125)
    norm_gain = jnp.clip(1.0 + 0.18 * jax.random.normal(key_of[9], (D,), jnp.float32), 0.1, 1.9)
    routes_keys = jax.random.split(jax.random.fold_in(key_of[10], 1), TOKEN_TOTAL // TOK_DEV)
    routes_turns = jax.random.permutation(jax.random.fold_in(key_of[10], 3), TOKEN_TOTAL // TOK_DEV)
    routes = jax.vmap(lambda own, number: deal_out(jax.random.fold_in(key_of[10], 2), own, number, TOK_DEV, EXPERTS, TOP, CAP, 1))(routes_keys, routes_turns).reshape((TOKEN_TOTAL, TOP))
    route_weights = jnp.clip(jnp.exp(math.log(1.0) - 2.3025851 * jax.random.uniform(key_of[11], (TOKEN_TOTAL, TOP), jnp.float32) ** shard_levels(key_of[11], (TOKEN_TOTAL, TOP), ((0, 32),), -0.2, 0.2)), 0.1, 1.0)
    expert_gate = normal_values(key_of[12], (2 * EXPERTS, FFH, D), D ** -0.5, 0.125, ((0, 32),))
    expert_up = normal_values(key_of[13], (2 * EXPERTS, FFH, D), D ** -0.5, 0.125, ((0, 32),))
    expert_down = normal_values(key_of[14], (2 * EXPERTS, FFH, D), FFE ** -0.5, 0.1875, ((0, 32),))
    return {"residual_in": residual_in, "queries": queries, "suffix_key_rows": suffix_key_rows, "suffix_value_rows": suffix_value_rows, "cached_prefix_keys": cached_prefix_keys, "cached_prefix_values": cached_prefix_values, "suffix_length_list": suffix_length_list, "prefix_read_flags": prefix_read_flags, "attn_out_weight": attn_out_weight, "norm_gain": norm_gain, "routes": routes, "route_weights": route_weights, "expert_gate": expert_gate, "expert_up": expert_up, "expert_down": expert_down}


def group_attention(packed_rows):
    query_rows, suffix_k, suffix_v, prefix_k, prefix_v, lengths, flags = packed_rows
    positions = jnp.arange(SUFFIX_TOKENS, dtype=jnp.int32)
    bounds = jnp.cumsum(lengths, dtype=jnp.int32)
    segment = lax.optimization_barrier(jnp.sum((positions[:, None] >= bounds[None, :]).astype(jnp.int32), axis=1))
    request_ids = jnp.arange(REQS, dtype=jnp.int32)
    reads = lax.optimization_barrier(jnp.sum(jnp.where(segment[:, None] == request_ids[None, :], flags[None, :], 0), axis=1)) > 0
    same_request = (segment[:, None] == segment[None, :]) & (positions[None, :] <= positions[:, None])
    visible = jnp.concatenate([jnp.broadcast_to(reads[:, None], (SUFFIX_TOKENS, PREFIX_TOKENS)), same_request], axis=1)
    all_keys = jnp.concatenate([prefix_k, suffix_k], axis=0)
    all_values = jnp.concatenate([prefix_v, suffix_v], axis=0)
    score_scale = 1.0 / math.sqrt(HEAD_SIZE)

    def head_output(head):
        kv_head = head // GRP
        query_head = lax.dynamic_slice_in_dim(query_rows, head * HEAD_SIZE, HEAD_SIZE, 1)
        key_head = lax.dynamic_slice_in_dim(all_keys, kv_head * HEAD_SIZE, HEAD_SIZE, 1)
        value_head = lax.dynamic_slice_in_dim(all_values, kv_head * HEAD_SIZE, HEAD_SIZE, 1)
        scores = jnp.dot(query_head, key_head.T, preferred_element_type=jnp.float32) * score_scale
        scores = jnp.where(visible, scores, -jnp.inf)
        row_max = lax.optimization_barrier(jnp.max(scores, axis=1, keepdims=True))
        weights = jnp.where(visible, jnp.exp(scores - row_max), 0.0)
        totals = lax.optimization_barrier(jnp.sum(weights, axis=1, keepdims=True))
        weighted = jnp.dot(weights.astype(jnp.bfloat16), value_head, preferred_element_type=jnp.float32)
        return weighted / totals
    per_head = lax.map(head_output, jnp.arange(QUERY_HEADS, dtype=jnp.int32))
    return jnp.transpose(per_head, (1, 0, 2)).reshape(SUFFIX_TOKENS, QUERY_HEADS * HEAD_SIZE)

def reference(residual_in, queries, suffix_key_rows, suffix_value_rows, cached_prefix_keys, cached_prefix_values, suffix_length_list, prefix_read_flags, attn_out_weight, norm_gain, routes, route_weights, expert_gate, expert_up, expert_down):
    packed_rows = (queries.reshape(N_GROUP, SUFFIX_TOKENS, QUERY_HEADS * HEAD_SIZE), suffix_key_rows.reshape(N_GROUP, SUFFIX_TOKENS, KEY_VALUE_HEADS * HEAD_SIZE), suffix_value_rows.reshape(N_GROUP, SUFFIX_TOKENS, KEY_VALUE_HEADS * HEAD_SIZE), cached_prefix_keys.reshape(N_GROUP, PREFIX_TOKENS, KEY_VALUE_HEADS * HEAD_SIZE), cached_prefix_values.reshape(N_GROUP, PREFIX_TOKENS, KEY_VALUE_HEADS * HEAD_SIZE), suffix_length_list, prefix_read_flags)
    context = lax.map(group_attention, packed_rows).reshape(TOKEN_TOTAL, QUERY_HEADS * HEAD_SIZE).astype(jnp.bfloat16)
    hidden = residual_in.astype(jnp.float32) + jnp.dot(context, attn_out_weight, preferred_element_type=jnp.float32)
    mean_square = lax.optimization_barrier(jnp.mean(hidden * hidden, axis=1, keepdims=True))
    normed = (hidden * lax.rsqrt(mean_square + 1e-05) * norm_gain).astype(jnp.bfloat16)
    flat_routes = routes.reshape(-1)
    token_ids = jnp.arange(TOKEN_TOTAL * TOP, dtype=jnp.int32) // TOP
    block_ids = token_ids // TOK_DEV
    one_hot = (flat_routes[:, None] == jnp.arange(EXPERTS, dtype=jnp.int32)[None, :]).astype(jnp.int32)
    running = jnp.cumsum(one_hot.reshape(DEVICES, TOK_DEV * TOP, EXPERTS), axis=1, dtype=jnp.int32)
    running = running.reshape(TOKEN_TOTAL * TOP, EXPERTS)
    slot_rank = lax.optimization_barrier(jnp.sum(one_hot * running, axis=1)) - 1
    targets = flat_routes * (DEVICES * CAP) + block_ids * CAP + slot_rank
    norm_weights = route_weights / lax.optimization_barrier(jnp.sum(route_weights, axis=1, keepdims=True))
    table_tokens = jnp.full((EXPERTS * DEVICES * CAP,), TOKEN_TOTAL, jnp.int32).at[targets].set(token_ids)
    table_tokens = table_tokens.reshape(EXPERTS, DEVICES * CAP)
    table_weights = jnp.zeros((EXPERTS * DEVICES * CAP,), jnp.float32).at[targets].set(norm_weights.reshape(-1))
    table_weights = table_weights.reshape(EXPERTS, DEVICES * CAP)
    padded = jnp.concatenate([normed, jnp.zeros((1, D), jnp.bfloat16)], axis=0)

    def expert_step(accum, inputs):
        row_ids, row_weights, gate_pair, up_pair, down_pair = inputs
        picked_rows = padded[row_ids]
        partials = []
        for half_index in range(2):
            gate_act = jnp.dot(picked_rows, gate_pair[half_index].T, preferred_element_type=jnp.float32)
            up_act = jnp.dot(picked_rows, up_pair[half_index].T, preferred_element_type=jnp.float32)
            hidden_act = (jax.nn.silu(gate_act) * up_act).astype(jnp.bfloat16)
            partials.append(jnp.dot(hidden_act, down_pair[half_index], preferred_element_type=jnp.float32).astype(jnp.bfloat16))
        combined = (partials[0].astype(jnp.float32) + partials[1].astype(jnp.float32)).astype(jnp.bfloat16)
        accum = accum.at[row_ids].add(row_weights[:, None] * combined.astype(jnp.float32), mode='drop')
        return (accum, None)
    expert_sum, unused = lax.scan(expert_step, jnp.zeros((TOKEN_TOTAL, D), jnp.float32), (table_tokens, table_weights, expert_gate.reshape(EXPERTS, 2, FFH, D), expert_up.reshape(EXPERTS, 2, FFH, D), expert_down.reshape(EXPERTS, 2, FFH, D)))
    return (hidden + expert_sum).astype(jnp.bfloat16)
```

```python
import math

import jax
import jax.numpy as jnp
from jax import lax
from jax.sharding import PartitionSpec as P

QUERY_HEADS = 20
KEY_VALUE_HEADS = 4
HEAD_SIZE = 128
TOP = 6
REQS = 8


def segment_of(positions, bounds):
    return jnp.sum((positions[:, None] >= bounds[None, :]).astype(jnp.int32), axis=1)


def per_device(
    residual_in,
    queries,
    suffix_key_rows,
    suffix_value_rows,
    cached_prefix_keys,
    cached_prefix_values,
    suffix_length_list,
    prefix_read_flags,
    attn_out_weight,
    norm_gain,
    routes,
    route_weights,
    expert_gate,
    expert_up,
    expert_down,
):
    token_rows = queries.shape[0]
    model_width = residual_in.shape[1]
    group_width = QUERY_HEADS // KEY_VALUE_HEADS
    my_group = lax.axis_index("group")
    my_place = lax.axis_index("expert")
    lengths_here = lax.dynamic_index_in_dim(suffix_length_list, my_group, 0, keepdims=False)
    flags_here = lax.dynamic_index_in_dim(prefix_read_flags, my_group, 0, keepdims=False)
    bounds = jnp.cumsum(lengths_here, dtype=jnp.int32)
    query_pos = my_place * token_rows + jnp.arange(token_rows, dtype=jnp.int32)
    query_seg = segment_of(query_pos, bounds)
    request_ids = jnp.arange(REQS, dtype=jnp.int32)
    query_reads = (
        jnp.sum(
            jnp.where(query_seg[:, None] == request_ids[None, :], flags_here[None, :], 0), axis=1
        )
        > 0
    )
    query_head_count = queries.reshape(token_rows, KEY_VALUE_HEADS, group_width, HEAD_SIZE)
    score_scale = 1.0 / math.sqrt(HEAD_SIZE)

    def attend(state_now, pieces, visible):
        running_max, running_sum, weighted = state_now
        key_portion, value_portion = pieces
        count_of_rows = key_portion.shape[0]
        key_row_block = key_portion.reshape(count_of_rows, KEY_VALUE_HEADS, HEAD_SIZE)
        value_row_block = value_portion.reshape(count_of_rows, KEY_VALUE_HEADS, HEAD_SIZE)
        scores = (
            jnp.einsum(
                "tkgd,skd->tkgs",
                query_head_count,
                key_row_block,
                preferred_element_type=jnp.float32,
            )
            * score_scale
        )
        seen = visible[:, None, None, :]
        scores = jnp.where(seen, scores, -jnp.inf)
        new_max = jnp.maximum(running_max, jnp.max(scores, axis=3))
        weights = jnp.where(seen, jnp.exp(scores - new_max[..., None]), 0.0)
        factor = jnp.exp(running_max - new_max)
        running_sum = running_sum * factor + jnp.sum(weights, axis=3)
        weighted = weighted * factor[..., None] + jnp.einsum(
            "tkgs,skd->tkgd",
            weights.astype(jnp.bfloat16),
            value_row_block,
            preferred_element_type=jnp.float32,
        )
        return (new_max, running_sum, weighted)

    start_state = (
        jnp.full((token_rows, KEY_VALUE_HEADS, group_width), -1e30, jnp.float32),
        jnp.zeros((token_rows, KEY_VALUE_HEADS, group_width), jnp.float32),
        jnp.zeros((token_rows, KEY_VALUE_HEADS, group_width, HEAD_SIZE), jnp.float32),
    )
    key_width = cached_prefix_keys.shape[1]
    prefix_pair = lax.all_gather(
        jnp.concatenate([cached_prefix_keys, cached_prefix_values], axis=1),
        "expert",
        axis=0,
        tiled=True,
    )
    suffix_pair = lax.all_gather(
        jnp.concatenate([suffix_key_rows, suffix_value_rows], axis=1),
        "expert",
        axis=0,
        tiled=True,
    )
    pieces = (prefix_pair[:, :key_width], prefix_pair[:, key_width:])
    visible = jnp.broadcast_to(query_reads[:, None], (token_rows, pieces[0].shape[0]))
    state_now = attend(start_state, pieces, visible)
    pieces = (suffix_pair[:, :key_width], suffix_pair[:, key_width:])
    key_pos = jnp.arange(pieces[0].shape[0], dtype=jnp.int32)
    key_seg = segment_of(key_pos, bounds)
    visible = (query_seg[:, None] == key_seg[None, :]) & (key_pos[None, :] <= query_pos[:, None])
    state_now = attend(state_now, pieces, visible)
    context = (
        (state_now[2] / state_now[1][..., None])
        .reshape(token_rows, QUERY_HEADS * HEAD_SIZE)
        .astype(jnp.bfloat16)
    )
    hidden = residual_in.astype(jnp.float32) + jnp.dot(
        context, attn_out_weight, preferred_element_type=jnp.float32
    )
    mean_square = jnp.mean(hidden * hidden, axis=1, keepdims=True)
    normed = (hidden * lax.rsqrt(mean_square + 1e-05) * norm_gain).astype(jnp.bfloat16)
    experts = lax.axis_size("group") * lax.axis_size("expert") // 2
    capacity = 2 * ((2 * token_rows * TOP + 3 * experts - 1) // (3 * experts))
    flat_routes = routes.reshape(-1)
    one_hot = (flat_routes[:, None] == jnp.arange(experts, dtype=jnp.int32)[None, :]).astype(
        jnp.int32
    )
    slot_rank = jnp.sum(one_hot * jnp.cumsum(one_hot, axis=0, dtype=jnp.int32), axis=1) - 1
    slot_index = flat_routes * capacity + slot_rank
    slot_ids = jnp.arange(experts * capacity, dtype=jnp.int32)
    dispatch_map = jnp.any(
        slot_index.reshape(token_rows, TOP)[None, :, :] == slot_ids[:, None, None], axis=2
    )
    buffer = jnp.dot(
        dispatch_map.astype(jnp.bfloat16), normed, preferred_element_type=jnp.float32
    ).astype(jnp.bfloat16)
    local_gate = expert_gate[0]
    local_up = expert_up[0]
    local_down = expert_down[0]
    half_rows = capacity // 2
    pairs = [(i, i ^ 1) for i in range(lax.axis_size("expert"))]

    def half_expert(rows):
        gate_act = lax.dot_general(
            rows, local_gate, (((1,), (1,)), ((), ())), preferred_element_type=jnp.float32
        )
        up_act = lax.dot_general(
            rows, local_up, (((1,), (1,)), ((), ())), preferred_element_type=jnp.float32
        )
        hidden_act = (jax.nn.silu(gate_act) * up_act).astype(jnp.bfloat16)
        return jnp.dot(hidden_act, local_down, preferred_element_type=jnp.float32).astype(
            jnp.bfloat16
        )

    sending = buffer.reshape(2 * experts, half_rows, model_width)
    arrived = lax.all_to_all(sending, ("group", "expert"), split_axis=0, concat_axis=0, tiled=True)
    own_rows = arrived.reshape(2 * experts * half_rows, model_width)
    pair_rows = lax.ppermute(own_rows, "expert", pairs)
    partial_pair = half_expert(pair_rows)
    from_pair = lax.ppermute(partial_pair, "expert", pairs)
    partial_own = half_expert(own_rows)
    combined = (partial_own.astype(jnp.float32) + from_pair.astype(jnp.float32)).astype(
        jnp.bfloat16
    )
    results = lax.all_to_all(
        combined.reshape(2 * experts, half_rows, model_width),
        ("group", "expert"),
        split_axis=0,
        concat_axis=0,
        tiled=True,
    ).reshape(experts * capacity, model_width)
    norm_weights = route_weights / jnp.sum(route_weights, axis=1, keepdims=True)
    mix_map = jnp.sum(
        jnp.where(
            slot_index.reshape(token_rows, TOP)[:, :, None] == slot_ids[None, None, :],
            norm_weights[:, :, None],
            0.0,
        ),
        axis=1,
    )
    mix_high = mix_map.astype(jnp.bfloat16)
    mix_low = (mix_map - mix_high.astype(jnp.float32)).astype(jnp.bfloat16)
    mixed = jnp.dot(mix_high, results, preferred_element_type=jnp.float32) + jnp.dot(
        mix_low, results, preferred_element_type=jnp.float32
    )
    return (hidden + mixed).astype(jnp.bfloat16)


def solution(mesh):
    in_specs = (
        P(("group", "expert"), None),
        P(("group", "expert"), None),
        P(("group", "expert"), None),
        P(("group", "expert"), None),
        P(("group", "expert"), None),
        P(("group", "expert"), None),
        P(),
        P(),
        P(),
        P(),
        P(("group", "expert"), None),
        P(("group", "expert"), None),
        P(("group", "expert"), None, None),
        P(("group", "expert"), None, None),
        P(("group", "expert"), None, None),
    )
    out_specs = P(("group", "expert"), None)
    return jax.shard_map(
        per_device, mesh=mesh, in_specs=in_specs, out_specs=out_specs, check_vma=False
    )
```

```python
import math

import jax
import jax.numpy as jnp
from jax import lax
from jax.sharding import PartitionSpec as P

QUERY_HEADS = 20
KEY_VALUE_HEADS = 4
HEAD_SIZE = 128
TOP = 6
REQS = 8


def segment_of(positions, bounds):
    return jnp.sum((positions[:, None] >= bounds[None, :]).astype(jnp.int32), axis=1)


def per_device(
    residual_in,
    queries,
    suffix_key_rows,
    suffix_value_rows,
    cached_prefix_keys,
    cached_prefix_values,
    suffix_length_list,
    prefix_read_flags,
    attn_out_weight,
    norm_gain,
    routes,
    route_weights,
    expert_gate,
    expert_up,
    expert_down,
):
    token_rows = queries.shape[0]
    model_width = residual_in.shape[1]
    group_width = QUERY_HEADS // KEY_VALUE_HEADS
    my_group = lax.axis_index("group")
    my_place = lax.axis_index("expert")
    lengths_here = lax.dynamic_index_in_dim(suffix_length_list, my_group, 0, keepdims=False)
    flags_here = lax.dynamic_index_in_dim(prefix_read_flags, my_group, 0, keepdims=False)
    bounds = jnp.cumsum(lengths_here, dtype=jnp.int32)
    query_pos = my_place * token_rows + jnp.arange(token_rows, dtype=jnp.int32)
    query_seg = segment_of(query_pos, bounds)
    request_ids = jnp.arange(REQS, dtype=jnp.int32)
    query_reads = (
        jnp.sum(
            jnp.where(query_seg[:, None] == request_ids[None, :], flags_here[None, :], 0), axis=1
        )
        > 0
    )
    query_head_count = queries.reshape(token_rows, KEY_VALUE_HEADS, group_width, HEAD_SIZE)
    score_scale = 1.0 / math.sqrt(HEAD_SIZE)

    def attend(state_now, pieces, visible):
        running_max, running_sum, weighted = state_now
        key_portion, value_portion = pieces
        count_of_rows = key_portion.shape[0]
        key_row_block = key_portion.reshape(count_of_rows, KEY_VALUE_HEADS, HEAD_SIZE)
        value_row_block = value_portion.reshape(count_of_rows, KEY_VALUE_HEADS, HEAD_SIZE)
        scores = (
            jnp.einsum(
                "tkgd,skd->tkgs",
                query_head_count,
                key_row_block,
                preferred_element_type=jnp.float32,
            )
            * score_scale
        )
        seen = visible[:, None, None, :]
        scores = jnp.where(seen, scores, -jnp.inf)
        new_max = jnp.maximum(running_max, jnp.max(scores, axis=3))
        weights = jnp.where(seen, jnp.exp(scores - new_max[..., None]), 0.0)
        factor = jnp.exp(running_max - new_max)
        running_sum = running_sum * factor + jnp.sum(weights, axis=3)
        weighted = weighted * factor[..., None] + jnp.einsum(
            "tkgs,skd->tkgd",
            weights.astype(jnp.bfloat16),
            value_row_block,
            preferred_element_type=jnp.float32,
        )
        return (new_max, running_sum, weighted)

    start_state = (
        jnp.full((token_rows, KEY_VALUE_HEADS, group_width), -1e30, jnp.float32),
        jnp.zeros((token_rows, KEY_VALUE_HEADS, group_width), jnp.float32),
        jnp.zeros((token_rows, KEY_VALUE_HEADS, group_width, HEAD_SIZE), jnp.float32),
    )
    norm_weights = route_weights / jnp.sum(route_weights, axis=1, keepdims=True)
    line_info = lax.all_gather(
        jnp.concatenate([routes.T.astype(jnp.float32), norm_weights.T], axis=0), "expert", axis=0
    )
    key_width = cached_prefix_keys.shape[1]
    prefix_pair = lax.all_gather(
        jnp.concatenate([cached_prefix_keys, cached_prefix_values], axis=1),
        "expert",
        axis=0,
        tiled=True,
    )
    suffix_pair = lax.all_gather(
        jnp.concatenate([suffix_key_rows, suffix_value_rows], axis=1),
        "expert",
        axis=0,
        tiled=True,
    )
    pieces = (prefix_pair[:, :key_width], prefix_pair[:, key_width:])
    visible = jnp.broadcast_to(query_reads[:, None], (token_rows, pieces[0].shape[0]))
    state_now = attend(start_state, pieces, visible)
    pieces = (suffix_pair[:, :key_width], suffix_pair[:, key_width:])
    key_pos = jnp.arange(pieces[0].shape[0], dtype=jnp.int32)
    key_seg = segment_of(key_pos, bounds)
    visible = (query_seg[:, None] == key_seg[None, :]) & (key_pos[None, :] <= query_pos[:, None])
    state_now = attend(state_now, pieces, visible)
    context = (
        (state_now[2] / state_now[1][..., None])
        .reshape(token_rows, QUERY_HEADS * HEAD_SIZE)
        .astype(jnp.bfloat16)
    )
    hidden = residual_in.astype(jnp.float32) + jnp.dot(
        context, attn_out_weight, preferred_element_type=jnp.float32
    )
    mean_square = jnp.mean(hidden * hidden, axis=1, keepdims=True)
    normed = (hidden * lax.rsqrt(mean_square + 1e-05) * norm_gain).astype(jnp.bfloat16)
    group_count = lax.axis_size("group")
    place_count = lax.axis_size("expert") // 2
    experts = group_count * place_count
    capacity = 2 * ((2 * token_rows * TOP + 3 * experts - 1) // (3 * experts))
    my_spot = my_place // 2
    my_core = my_place % 2

    line = line_info.reshape(place_count, 2, 2 * TOP, token_rows)
    line = lax.dynamic_index_in_dim(line, my_core, 1, keepdims=False)
    line = jnp.stack(
        [
            lax.dynamic_index_in_dim(line, my_spot ^ step, 0, keepdims=False)
            for step in range(place_count)
        ]
    )
    experts_here = (
        jnp.bitwise_xor(my_group, jnp.arange(group_count, dtype=jnp.int32)) * place_count + my_spot
    ).astype(jnp.float32)
    named = line[:, None, :TOP, :] == experts_here[None, :, None, None]
    picked = jnp.any(named, axis=2)
    picked_weight = jnp.sum(jnp.where(named, line[:, None, TOP:, :], 0.0), axis=2)
    token_ids = jnp.arange(token_rows, dtype=jnp.int32)
    upper = (token_ids[:, None] <= token_ids[None, :]).astype(jnp.bfloat16)
    rank = jnp.dot(
        picked.astype(jnp.bfloat16).reshape(place_count * group_count, token_rows),
        upper,
        preferred_element_type=jnp.float32,
    ).reshape(place_count, group_count, token_rows)
    slot_ids = jnp.arange(1, capacity + 1, dtype=jnp.int32).astype(jnp.float32)
    slot_map = picked[:, :, None, :] & (rank[:, :, None, :] == slot_ids[None, None, :, None])
    slots = group_count * capacity
    pick_map = slot_map.astype(jnp.bfloat16).reshape(place_count, slots, token_rows)
    mix_map = jnp.where(slot_map, picked_weight[:, :, None, :], 0.0)
    mix_map = mix_map.reshape(place_count, slots, token_rows)
    mix_high = mix_map.astype(jnp.bfloat16)
    mix_low = (mix_map - mix_high.astype(jnp.float32)).astype(jnp.bfloat16)

    local_gate = expert_gate[0]
    local_up = expert_up[0]
    local_down = expert_down[0]

    def swap(rows, axis, distance):
        pairs = [(i, i ^ distance) for i in range(lax.axis_size(axis))]
        return lax.ppermute(rows, axis, pairs)

    def half_expert(rows):
        gate_act = lax.dot_general(
            rows, local_gate, (((1,), (1,)), ((), ())), preferred_element_type=jnp.float32
        )
        up_act = lax.dot_general(
            rows, local_up, (((1,), (1,)), ((), ())), preferred_element_type=jnp.float32
        )
        hidden_act = (jax.nn.silu(gate_act) * up_act).astype(jnp.bfloat16)
        return jnp.dot(hidden_act, local_down, preferred_element_type=jnp.float32).astype(
            jnp.bfloat16
        )

    def over_groups(rows):
        parts = [rows[:capacity]]
        for distance in range(1, group_count):
            part = rows[distance * capacity : (distance + 1) * capacity]
            parts.append(swap(part, "group", distance))
        return jnp.concatenate(parts, axis=0)

    blocks = [normed] + [swap(normed, "expert", 2 * step) for step in range(1, place_count)]
    total = hidden
    for step in range(place_count):
        rows = jnp.dot(
            pick_map[step], blocks[step], preferred_element_type=jnp.float32
        ).astype(jnp.bfloat16)
        rows = over_groups(rows)
        partial_pair = half_expert(swap(rows, "expert", 1))
        partial_own = half_expert(rows)
        combined = (
            partial_own.astype(jnp.float32) + swap(partial_pair, "expert", 1).astype(jnp.float32)
        ).astype(jnp.bfloat16)
        outs = over_groups(combined)
        contract = (((0,), (0,)), ((), ()))
        piece = lax.dot_general(
            mix_high[step], outs, contract, preferred_element_type=jnp.float32
        ) + lax.dot_general(mix_low[step], outs, contract, preferred_element_type=jnp.float32)
        if step > 0:
            piece = swap(piece.astype(jnp.bfloat16), "expert", 2 * step).astype(jnp.float32)
        total = total + piece
    return total.astype(jnp.bfloat16)


def solution(mesh):
    in_specs = (
        P(("group", "expert"), None),
        P(("group", "expert"), None),
        P(("group", "expert"), None),
        P(("group", "expert"), None),
        P(("group", "expert"), None),
        P(("group", "expert"), None),
        P(),
        P(),
        P(),
        P(),
        P(("group", "expert"), None),
        P(("group", "expert"), None),
        P(("group", "expert"), None, None),
        P(("group", "expert"), None, None),
        P(("group", "expert"), None, None),
    )
    out_specs = P(("group", "expert"), None)
    return jax.shard_map(
        per_device, mesh=mesh, in_specs=in_specs, out_specs=out_specs, check_vma=False
    )
```

```python
import math

import jax
import jax.numpy as jnp
from jax import lax
from jax.sharding import PartitionSpec as P

QUERY_HEADS = 20
KEY_VALUE_HEADS = 4
HEAD_SIZE = 128
TOP = 6
REQS = 8


def segment_of(positions, bounds):
    return jnp.sum((positions[:, None] >= bounds[None, :]).astype(jnp.int32), axis=1)


def per_device(
    residual_in,
    queries,
    suffix_key_rows,
    suffix_value_rows,
    cached_prefix_keys,
    cached_prefix_values,
    suffix_length_list,
    prefix_read_flags,
    attn_out_weight,
    norm_gain,
    routes,
    route_weights,
    expert_gate,
    expert_up,
    expert_down,
):
    token_rows = queries.shape[0]
    model_width = residual_in.shape[1]
    group_width = QUERY_HEADS // KEY_VALUE_HEADS
    my_group = lax.axis_index("group")
    my_place = lax.axis_index("expert")
    lengths_here = lax.dynamic_index_in_dim(suffix_length_list, my_group, 0, keepdims=False)
    flags_here = lax.dynamic_index_in_dim(prefix_read_flags, my_group, 0, keepdims=False)
    bounds = jnp.cumsum(lengths_here, dtype=jnp.int32)
    query_pos = my_place * token_rows + jnp.arange(token_rows, dtype=jnp.int32)
    query_seg = segment_of(query_pos, bounds)
    request_ids = jnp.arange(REQS, dtype=jnp.int32)
    query_reads = (
        jnp.sum(
            jnp.where(query_seg[:, None] == request_ids[None, :], flags_here[None, :], 0), axis=1
        )
        > 0
    )
    query_head_count = queries.reshape(token_rows, KEY_VALUE_HEADS, group_width, HEAD_SIZE)
    score_scale = 1.0 / math.sqrt(HEAD_SIZE)

    def attend(state_now, pieces, visible):
        running_max, running_sum, weighted = state_now
        key_portion, value_portion = pieces
        count_of_rows = key_portion.shape[0]
        key_row_block = key_portion.reshape(count_of_rows, KEY_VALUE_HEADS, HEAD_SIZE)
        value_row_block = value_portion.reshape(count_of_rows, KEY_VALUE_HEADS, HEAD_SIZE)
        scores = (
            jnp.einsum(
                "tkgd,skd->tkgs",
                query_head_count,
                key_row_block,
                preferred_element_type=jnp.float32,
            )
            * score_scale
        )
        seen = visible[:, None, None, :]
        scores = jnp.where(seen, scores, -jnp.inf)
        new_max = jnp.maximum(running_max, jnp.max(scores, axis=3))
        weights = jnp.where(seen, jnp.exp(scores - new_max[..., None]), 0.0)
        factor = jnp.exp(running_max - new_max)
        running_sum = running_sum * factor + jnp.sum(weights, axis=3)
        weighted = weighted * factor[..., None] + jnp.einsum(
            "tkgs,skd->tkgd",
            weights.astype(jnp.bfloat16),
            value_row_block,
            preferred_element_type=jnp.float32,
        )
        return (new_max, running_sum, weighted)

    start_state = (
        jnp.full((token_rows, KEY_VALUE_HEADS, group_width), -1e30, jnp.float32),
        jnp.zeros((token_rows, KEY_VALUE_HEADS, group_width), jnp.float32),
        jnp.zeros((token_rows, KEY_VALUE_HEADS, group_width, HEAD_SIZE), jnp.float32),
    )
    norm_weights = route_weights / jnp.sum(route_weights, axis=1, keepdims=True)
    line_info = lax.all_gather(
        jnp.concatenate([routes.T.astype(jnp.float32), norm_weights.T], axis=0), "expert", axis=0
    )
    key_width = cached_prefix_keys.shape[1]
    prefix_pair = lax.all_gather(
        jnp.concatenate([cached_prefix_keys, cached_prefix_values], axis=1),
        "expert",
        axis=0,
        tiled=True,
    )
    suffix_pair = lax.all_gather(
        jnp.concatenate([suffix_key_rows, suffix_value_rows], axis=1),
        "expert",
        axis=0,
        tiled=True,
    )
    pieces = (prefix_pair[:, :key_width], prefix_pair[:, key_width:])
    visible = jnp.broadcast_to(query_reads[:, None], (token_rows, pieces[0].shape[0]))
    state_now = attend(start_state, pieces, visible)
    pieces = (suffix_pair[:, :key_width], suffix_pair[:, key_width:])
    key_pos = jnp.arange(pieces[0].shape[0], dtype=jnp.int32)
    key_seg = segment_of(key_pos, bounds)
    visible = (query_seg[:, None] == key_seg[None, :]) & (key_pos[None, :] <= query_pos[:, None])
    state_now = attend(state_now, pieces, visible)
    context = (
        (state_now[2] / state_now[1][..., None])
        .reshape(token_rows, QUERY_HEADS * HEAD_SIZE)
        .astype(jnp.bfloat16)
    )
    hidden = residual_in.astype(jnp.float32) + jnp.dot(
        context, attn_out_weight, preferred_element_type=jnp.float32
    )
    mean_square = jnp.mean(hidden * hidden, axis=1, keepdims=True)
    normed = (hidden * lax.rsqrt(mean_square + 1e-05) * norm_gain).astype(jnp.bfloat16)
    group_count = lax.axis_size("group")
    place_count = lax.axis_size("expert") // 2
    experts = group_count * place_count
    capacity = 2 * ((2 * token_rows * TOP + 3 * experts - 1) // (3 * experts))
    my_spot = my_place // 2
    my_core = my_place % 2

    line = line_info.reshape(place_count, 2, 2 * TOP, token_rows)
    line = lax.dynamic_index_in_dim(line, my_core, 1, keepdims=False)
    line = jnp.stack(
        [
            lax.dynamic_index_in_dim(line, my_spot ^ step, 0, keepdims=False)
            for step in range(place_count)
        ]
    )
    experts_here = (
        jnp.bitwise_xor(my_group, jnp.arange(group_count, dtype=jnp.int32)) * place_count + my_spot
    ).astype(jnp.float32)
    named = line[:, None, :TOP, :] == experts_here[None, :, None, None]
    picked = jnp.any(named, axis=2)
    picked_weight = jnp.sum(jnp.where(named, line[:, None, TOP:, :], 0.0), axis=2)
    token_ids = jnp.arange(token_rows, dtype=jnp.int32)
    upper = (token_ids[:, None] <= token_ids[None, :]).astype(jnp.bfloat16)
    rank = jnp.dot(
        picked.astype(jnp.bfloat16).reshape(place_count * group_count, token_rows),
        upper,
        preferred_element_type=jnp.float32,
    ).reshape(place_count, group_count, token_rows)
    slot_ids = jnp.arange(1, capacity + 1, dtype=jnp.int32).astype(jnp.float32)
    slot_map = picked[:, :, None, :] & (rank[:, :, None, :] == slot_ids[None, None, :, None])
    slots = group_count * capacity
    pick_map = slot_map.astype(jnp.bfloat16).reshape(place_count, slots, token_rows)
    mix_map = jnp.where(slot_map, picked_weight[:, :, None, :], 0.0)
    mix_map = mix_map.reshape(place_count, slots, token_rows)
    mix_high = mix_map.astype(jnp.bfloat16)
    mix_low = (mix_map - mix_high.astype(jnp.float32)).astype(jnp.bfloat16)

    local_gate = expert_gate[0]
    local_up = expert_up[0]
    local_down = expert_down[0]

    def swap(rows, axis, distance):
        pairs = [(i, i ^ distance) for i in range(lax.axis_size(axis))]
        return lax.ppermute(rows, axis, pairs)

    def half_expert(rows):
        gate_act = lax.dot_general(
            rows, local_gate, (((1,), (1,)), ((), ())), preferred_element_type=jnp.float32
        )
        up_act = lax.dot_general(
            rows, local_up, (((1,), (1,)), ((), ())), preferred_element_type=jnp.float32
        )
        hidden_act = (jax.nn.silu(gate_act) * up_act).astype(jnp.bfloat16)
        return jnp.dot(hidden_act, local_down, preferred_element_type=jnp.float32).astype(
            jnp.bfloat16
        )

    def after(value, other):
        zero = jnp.minimum(jnp.abs(other[0, 0].astype(jnp.float32)), 0.0)
        return value + zero.astype(value.dtype)

    def over_groups(rows, wait_for=()):
        parts = [rows[:capacity]]
        for distance in range(1, group_count):
            part = rows[distance * capacity : (distance + 1) * capacity]
            parts.append(swap(part, "group", distance))
        for other in wait_for:
            parts[-1] = after(parts[-1], other)
        return jnp.concatenate(parts, axis=0)

    def pick(chosen_map, block):
        return jnp.dot(chosen_map, block, preferred_element_type=jnp.float32).astype(
            jnp.bfloat16
        )

    blocks = [normed] + [swap(normed, "expert", 2 * step) for step in range(1, place_count)]
    picked_rows = [pick(pick_map[step], blocks[step]) for step in range(2)]
    finished = []
    for step in range(place_count):
        rows = over_groups(picked_rows[step], picked_rows[step + 1 : step + 2])
        partial_pair = half_expert(swap(rows, "expert", 1))
        partial_own = half_expert(rows)
        finished.append(
            (
                partial_own.astype(jnp.float32)
                + swap(partial_pair, "expert", 1).astype(jnp.float32)
            ).astype(jnp.bfloat16)
        )
        if step + 2 < place_count:
            picked_rows.append(pick(after(pick_map[step + 2], finished[step]), blocks[step + 2]))
    total = hidden
    contract = (((0,), (0,)), ((), ()))
    for step in list(range(1, place_count)) + [0]:
        combined = finished[step]
        outs = over_groups(combined)
        piece = lax.dot_general(
            mix_high[step], outs, contract, preferred_element_type=jnp.float32
        ) + lax.dot_general(mix_low[step], outs, contract, preferred_element_type=jnp.float32)
        if step > 0:
            piece = swap(piece.astype(jnp.bfloat16), "expert", 2 * step).astype(jnp.float32)
        total = total + piece
    return total.astype(jnp.bfloat16)


def solution(mesh):
    in_specs = (
        P(("group", "expert"), None),
        P(("group", "expert"), None),
        P(("group", "expert"), None),
        P(("group", "expert"), None),
        P(("group", "expert"), None),
        P(("group", "expert"), None),
        P(),
        P(),
        P(),
        P(),
        P(("group", "expert"), None),
        P(("group", "expert"), None),
        P(("group", "expert"), None, None),
        P(("group", "expert"), None, None),
        P(("group", "expert"), None, None),
    )
    out_specs = P(("group", "expert"), None)
    return jax.shard_map(
        per_device, mesh=mesh, in_specs=in_specs, out_specs=out_specs, check_vma=False
    )
```
